32 devices in a mesh: tm: 8 (over z, x), space: 4 (over y, core).
Axes of the slice: x: 2, y: 2, z: 4, core: 2. Of those that a mesh axis runs over, the one named last changes fastest.
Arguments:
- guess: float32 [8, 5, 2, 32, 64, 128], P('tm', None, None, 'space'), may hold values from 0 to 1
- feed_rate: float32 [32, 64, 128], P('space'), may hold values from 0.05 to 0.5
- kill_rate: float32 [32, 64, 128], P('space'), may hold values from 0.05 to 0.5
Outputs:
- end_state: float32 [8, 2, 32, 64, 128], P('tm', None, 'space')
- next_nodes: float32 [8, 5, 2, 32, 64, 128], P('tm', None, None, 'space')
The draws below stay inside these ranges and needn't reach their ends.
All inputs are finite; a program needn't handle non-finite values.
Results may differ from the reference program's by a relative error of at most 0.00002.
Values sent between devices are 32-bit elements; how exact they have to be, the bound alone decides.
A program may use at most 64 MiB of HBM per device.

```python
import math
import jax
import jax.numpy as jnp
import numpy as np
from jax import lax

NY = 64
NZ = 128
NODES = 5
SWEEPS = 4
NX = 32
SLABS = 8


def steps_of(rng, dims, shards, least, high):
    gain = 1.0
    for position, parts in shards:
        steps = jax.random.uniform(jax.random.fold_in(jax.random.fold_in(rng, 6), position), (parts,), jnp.float32, least / len(shards), high / len(shards))
        gain = gain * jnp.repeat(jnp.exp(steps), dims[position] // parts).reshape((-1,) + (1,) * (len(dims) - 1 - position))
    return gain


def setup_inputs(seed: int = 0) -> dict:
    splits = jax.random.split(jax.random.key(seed), 4)
    return {
        "guess": jnp.clip(1.0 * jax.random.uniform(splits[0], (SLABS, NODES, 2, NX, NY, NZ), jnp.float32) ** steps_of(splits[0], (SLABS, NODES, 2, NX, NY, NZ), ((0, 8), (3, 4)), -0.2, 0.2), 0.0, 1.0),
        "feed_rate": jnp.clip(jnp.exp(math.log(0.5) - 2.3025851 * jax.random.uniform(splits[1], (NX, NY, NZ), jnp.float32) ** steps_of(splits[1], (NX, NY, NZ), ((0, 4),), -0.2, 0.2)), 0.05, 0.5),
        "kill_rate": jnp.clip(jnp.exp(math.log(0.5) - 2.3025851 * jax.random.uniform(splits[2], (NX, NY, NZ), jnp.float32) ** steps_of(splits[2], (NX, NY, NZ), ((0, 4),), -0.2, 0.2)), 0.05, 0.5),
    }


substrate_spread = 0.2
catalyst_spread = 0.1
slab_time = 0.5

def lobatto_table():
    spread_root = math.sqrt(3.0 / 7.0)
    node_times = [0.0, (1.0 - spread_root) / 2.0, 0.5, (1.0 + spread_root) / 2.0, 1.0]
    table = [[0.0] * 5 for blank in range(5)]
    for column in range(5):
        coeffs = [1.0]
        divisor = 1.0
        for other_node in range(5):
            if other_node != column:
                product = [0.0] * (len(coeffs) + 1)
                for power, entry in enumerate(coeffs):
                    product[power + 1] += entry
                    product[power] -= node_times[other_node] * entry
                coeffs = product
                divisor *= node_times[column] - node_times[other_node]
        for row_index in range(5):
            upper = node_times[row_index]
            total_sum = 0.0
            for power, entry in enumerate(coeffs):
                total_sum += entry / (power + 1) * upper ** (power + 1)
            table[row_index][column] = total_sum / divisor
    return (np.array(node_times), np.array(table))

def laplacian(fields):
    total = -6.0 * fields
    for axis_id in (-3, -2, -1):
        total = total + jnp.roll(fields, 1, axis_id) + jnp.roll(fields, -1, axis_id)
    return total

def reaction_rates(fields, laplace_terms, feed_rate, kill_rate):
    substrate = fields[..., 0, :, :, :]
    catalyst = fields[..., 1, :, :, :]
    reacting = substrate * catalyst * catalyst
    grow_sub = substrate_spread * laplace_terms[..., 0, :, :, :] - reacting + feed_rate * (1.0 - substrate)
    grow_cat = catalyst_spread * laplace_terms[..., 1, :, :, :] + reacting - (feed_rate + kill_rate) * catalyst
    return jnp.stack([grow_sub, grow_cat], axis=-4)

def combine(start_pair, rates_all, weights):
    increment = jnp.zeros_like(rates_all)
    for column in range(weights.shape[1]):
        scale_col = jnp.asarray(weights[:, column], jnp.float32).reshape((-1, 1, 1, 1, 1))
        increment = increment + scale_col * rates_all[column][None]
    return start_pair[None] + slab_time * increment

def reference(guess, feed_rate, kill_rate):
    node_times, weights = lobatto_table()

    def sweep_slab(slab_pair):
        node_fields, start_pair = slab_pair
        rates_all = reaction_rates(node_fields, laplacian(node_fields), feed_rate, kill_rate)
        return combine(start_pair, rates_all, weights)
    node_all = guess
    for sweep_index in range(SWEEPS):
        end_fields = node_all[:, -1]
        starts = jnp.concatenate([guess[:1, 0], end_fields[:-1]], axis=0)
        node_all = lax.map(sweep_slab, (node_all, starts))
    end_state = node_all[:, -1]
    last_pair = end_state[-1]
    seed_rate = reaction_rates(last_pair, laplacian(last_pair), feed_rate, kill_rate)
    offsets = jnp.asarray(node_times, jnp.float32).reshape((-1, 1, 1, 1, 1))
    next_one = last_pair[None] + slab_time * offsets * seed_rate[None]
    next_nodes = jnp.broadcast_to(next_one[None], (SLABS,) + next_one.shape)
    return (end_state, next_nodes)
```

```python
import functools
import math

import jax
import jax.numpy as jnp
import numpy as np
from jax import lax
from jax.experimental import pallas as pl
from jax.experimental.pallas import tpu as pltpu
from jax.sharding import PartitionSpec as P

SWEEPS = 4
LAG = 2

substrate_spread = 0.2
catalyst_spread = 0.1
slab_time = 0.5

MESH = pl.DeviceIdType.MESH


def lobatto_table():
    spread_root = math.sqrt(3.0 / 7.0)
    node_times = [0.0, (1.0 - spread_root) / 2.0, 0.5, (1.0 + spread_root) / 2.0, 1.0]
    table = [[0.0] * 5 for blank in range(5)]
    for column in range(5):
        coeffs = [1.0]
        divisor = 1.0
        for other_node in range(5):
            if other_node != column:
                product = [0.0] * (len(coeffs) + 1)
                for power, entry in enumerate(coeffs):
                    product[power + 1] += entry
                    product[power] -= node_times[other_node] * entry
                coeffs = product
                divisor *= node_times[column] - node_times[other_node]
        for row_index in range(5):
            upper = node_times[row_index]
            total_sum = 0.0
            for power, entry in enumerate(coeffs):
                total_sum += entry / (power + 1) * upper ** (power + 1)
            table[row_index][column] = total_sum / divisor
    return (np.array(node_times), np.array(table))


def rates(below, here, above, feed, drain):
    rows, lanes = here[0].shape

    def lap(i):
        w = here[i]
        around = (pltpu.roll(w, 1, 0) + pltpu.roll(w, rows - 1, 0)) + (
            pltpu.roll(w, 1, 1) + pltpu.roll(w, lanes - 1, 1)
        )
        return around + (below[i] + above[i]) - 6.0 * w

    s, c = here
    reacting = s * c * c
    grow_sub = substrate_spread * lap(0) - reacting + feed * (1.0 - s)
    grow_cat = catalyst_spread * lap(1) + reacting - drain * c
    return grow_sub, grow_cat


def kernel(
    slabs, blocks, weights,
    guess, feed_in, kill_in,
    end_out, last_out, rate_out,
    u, last, feed, drain, fbuf,
    load_sem, fixed_sem, tm_send, tm_recv, halo_send, halo_recv, cast_send, cast_recv,
):
    layers = guess.shape[2]
    rows = guess.shape[3]
    tm = lax.axis_index("tm")
    sp = lax.axis_index("space")
    left = lax.rem(sp + blocks - 1, blocks)
    right = lax.rem(sp + 1, blocks)
    top = slabs // 2 - 1
    a = tm // 2
    b = tm % 2
    source = tm == slabs - 1
    not_source = tm < slabs - 1
    primary = 1 - b

    def layer_of(c):
        half = c // 2
        odd = c % 2
        return half + odd * (layers - 1 - 2 * half)

    loads = [
        pltpu.make_async_copy(guess, u.at[0, :, :, pl.ds(1, layers)], load_sem.at[0]),
        pltpu.make_async_copy(feed_in, feed, load_sem.at[1]),
        pltpu.make_async_copy(kill_in, drain, load_sem.at[2]),
    ]
    for load in loads:
        load.start()

    def fixed(k):
        return pltpu.make_async_copy(guess.at[0], u.at[k, 0, :, pl.ds(1, layers)], fixed_sem.at[k - 1])

    @pl.when(tm == 0)
    def _():
        for k in range(1, SWEEPS + 1):
            fixed(k).start()

    barrier = pltpu.get_barrier_semaphore()
    for hop in (1, 2, slabs - 2, slabs - 1):
        pl.semaphore_signal(barrier, inc=1, device_id={"tm": lax.rem(tm + hop, slabs)}, device_id_type=MESH)
    for side in (left, right):
        pl.semaphore_signal(barrier, inc=1, device_id={"space": side}, device_id_type=MESH)
    pl.semaphore_wait(barrier, 6)

    def stream(k, c, src):
        return pltpu.make_async_remote_copy(
            src_ref=src,
            dst_ref=u.at[k + 1, 0, :, 1 + layer_of(c)],
            send_sem=tm_send.at[k, c],
            recv_sem=tm_recv.at[k, c],
            device_id={"tm": lax.rem(tm + 1, slabs)},
            device_id_type=MESH,
        )

    def halo(k, side, src):
        return pltpu.make_async_remote_copy(
            src_ref=src,
            dst_ref=u.at[k, :, :, (1 - side) * (layers + 1)],
            send_sem=halo_send.at[k, side],
            recv_sem=halo_recv.at[k, side],
            device_id={"space": left + side * (right - left)},
            device_id_type=MESH,
        )

    def own_edge(k, side):
        return u.at[k, :, :, 1 + side * (layers - 1)]

    halo(0, 0, guess.at[:, :, 0]).start()
    halo(0, 1, guess.at[:, :, layers - 1]).start()

    @pl.when(not_source)
    def _():
        @pl.loop(0, layers)
        def _(c):
            stream(0, c, guess.at[4, :, layer_of(c)]).start()

    for load in loads:
        load.wait()
    drain[...] = drain[...] + feed[...]

    @pl.when(tm == 0)
    def _():
        for k in range(1, SWEEPS + 1):
            fixed(k).wait()

    def arrive(k, c):
        @pl.when(c == 0)
        def _():
            halo(k, 1, own_edge(k, 1)).wait_recv()

        @pl.when(c == 1)
        def _():
            halo(k, 0, own_edge(k, 0)).wait_recv()

    def begin(k, c):
        @pl.when(tm > 0)
        def _():
            stream(k, c, u.at[k, 4, :, 1 + layer_of(c)]).wait_recv()

    def all_rates(k, i):
        f, d = feed[i], drain[i]
        for j in range(5):
            below, here, above = ((u[k, j, 0, i + n], u[k, j, 1, i + n]) for n in range(3))
            fbuf[j, 0], fbuf[j, 1] = rates(below, here, above, f, d)

    def step(k, i, nodes):
        @pl.loop(0, rows // 8)
        def _(r):
            at = pl.ds(pl.multiple_of(r * 8, 8), 8)
            for s in range(2):
                start = u[k + 1, 0, s, 1 + i, at]
                grown = [fbuf[j, s, at] for j in range(5)]
                for m in nodes:
                    total = grown[0] * weights[m][0]
                    for j in range(1, 5):
                        total = total + grown[j] * weights[m][j]
                    u[k + 1, m, s, 1 + i, at] = start + total

    @pl.loop(0, SWEEPS - 1)
    def _(k):
        @pl.loop(0, layers)
        def _(c):
            i = layer_of(c)
            arrive(k, c)
            all_rates(k, i)
            begin(k, c)
            step(k, i, (4, 1, 2, 3))

            @pl.when(not_source)
            def _():
                stream(k + 1, c, u.at[k + 1, 4, :, 1 + i]).start()

            @pl.when(c < 2)
            def _():
                halo(k + 1, c, own_edge(k + 1, c)).start()

    def cast(lane, c, species, target):
        at = last.at[species, 1 + layer_of(c)]
        return pltpu.make_async_remote_copy(
            src_ref=at,
            dst_ref=at,
            send_sem=cast_send.at[lane, c],
            recv_sem=cast_recv.at[species, c],
            device_id={"tm": target},
            device_id_type=MESH,
        )

    down_on = a > 0
    cross_on = (a < top) | source
    cross_species = primary + jnp.where(source, 1, 0)
    extra_on = tm == 2 * (top - 1)

    def down(c):
        return cast(0, c, primary, lax.rem(tm + slabs - 2, slabs))

    def cross(c):
        return cast(1, c, cross_species, tm + 1 - 2 * b)

    def extra(c):
        return cast(2, c, 0, lax.rem(tm + 2, slabs))

    def last_halo(side):
        return pltpu.make_async_remote_copy(
            src_ref=last.at[:, 1 + side * (layers - 1)],
            dst_ref=last.at[:, (1 - side) * (layers + 1)],
            send_sem=halo_send.at[SWEEPS, side],
            recv_sem=halo_recv.at[SWEEPS, side],
            device_id={"space": left + side * (right - left)},
            device_id_type=MESH,
        )

    @pl.loop(0, layers + LAG)
    def _(c):
        @pl.when(c < layers)
        def _():
            i = layer_of(c)
            arrive(SWEEPS - 1, c)
            all_rates(SWEEPS - 1, i)
            begin(SWEEPS - 1, c)
            step(SWEEPS - 1, i, (4,))
            end_out[:, i] = u[SWEEPS, 4, :, 1 + i]

            @pl.when(source)
            def _():
                last[:, 1 + i] = u[SWEEPS, 4, :, 1 + i]

            @pl.when(not_source)
            def _():
                cast(0, c, primary, tm).wait_recv()

            @pl.when(down_on)
            def _():
                down(c).start()

            @pl.when(cross_on)
            def _():
                cross(c).start()

        @pl.when(c >= LAG)
        def _():
            late = c - LAG

            @pl.when(not_source)
            def _():
                cast(0, late, 1 - primary, tm).wait_recv()

            @pl.when(extra_on)
            def _():
                extra(late).start()

            @pl.when(late < 2)
            def _():
                last_halo(late).start()

    last_halo(0).wait_recv()
    last_halo(1).wait_recv()

    @pl.loop(0, layers)
    def _(i):
        below, here, above = ((last[0, i + n], last[1, i + n]) for n in range(3))
        grow = rates(below, here, above, feed[i], drain[i])
        for s in range(2):
            last_out[s, i] = here[s]
            rate_out[s, i] = slab_time * grow[s]

    for k in range(SWEEPS):
        for side in range(2):
            halo(k, side, own_edge(k, side)).wait_send()
    last_halo(0).wait_send()
    last_halo(1).wait_send()

    @pl.loop(0, layers)
    def _(c):
        @pl.when(not_source)
        def _():
            for k in range(SWEEPS):
                stream(k, c, u.at[k, 4, :, 1 + layer_of(c)]).wait_send()

        @pl.when(down_on)
        def _():
            down(c).wait_send()

        @pl.when(cross_on)
        def _():
            cross(c).wait_send()

        @pl.when(extra_on)
        def _():
            extra(c).wait_send()


def shards(slabs, blocks, guess, feed_rate, kill_rate):
    node_times, table = lobatto_table()
    weights = [[float(np.float32(slab_time * w)) for w in row] for row in table]
    _, nodes, species, layers, rows, lanes = guess.shape
    pair = jax.ShapeDtypeStruct((species, layers, rows, lanes), jnp.float32)
    dma = pltpu.SemaphoreType.DMA
    end, last, rate = pl.pallas_call(
        functools.partial(kernel, slabs, blocks, weights),
        out_shape=(pair, pair, pair),
        in_specs=[pl.BlockSpec(memory_space=pl.ANY)] * 3,
        out_specs=(pl.BlockSpec(memory_space=pltpu.VMEM),) * 3,
        scratch_shapes=[
            pltpu.VMEM((SWEEPS + 1, nodes, species, layers + 2, rows, lanes), jnp.float32),
            pltpu.VMEM((species, layers + 2, rows, lanes), jnp.float32),
            pltpu.VMEM((layers, rows, lanes), jnp.float32),
            pltpu.VMEM((layers, rows, lanes), jnp.float32),
            pltpu.VMEM((nodes, species, rows, lanes), jnp.float32),
            dma((3,)),
            dma((SWEEPS,)),
            dma((SWEEPS, layers)),
            dma((SWEEPS, layers)),
            dma((SWEEPS + 1, 2)),
            dma((SWEEPS + 1, 2)),
            dma((3, layers)),
            dma((2, layers)),
        ],
        compiler_params=pltpu.CompilerParams(
            collective_id=0, has_side_effects=True, vmem_limit_bytes=40 * 1024 * 1024
        ),
    )(guess[0], feed_rate, kill_rate)
    offsets = jnp.asarray(node_times, jnp.float32).reshape((-1, 1, 1, 1, 1))
    next_one = last[None] + offsets * rate[None]
    return (end[None], next_one[None])


def solution(mesh):
    placed = (
        P("tm", None, None, "space", None, None),
        P("space", None, None),
        P("space", None, None),
    )
    return jax.shard_map(
        functools.partial(shards, mesh.shape["tm"], mesh.shape["space"]),
        mesh=mesh,
        in_specs=placed,
        out_specs=(P("tm", None, "space", None, None), P("tm", None, None, "space", None, None)),
        check_vma=False,
    )
```

```python
import functools
import math

import jax
import jax.numpy as jnp
import numpy as np
from jax import lax
from jax.experimental import pallas as pl
from jax.experimental.pallas import tpu as pltpu
from jax.sharding import PartitionSpec as P

SWEEPS = 4
LAG = 2

substrate_spread = 0.2
catalyst_spread = 0.1
slab_time = 0.5

MESH = pl.DeviceIdType.MESH


def lobatto_table():
    spread_root = math.sqrt(3.0 / 7.0)
    node_times = [0.0, (1.0 - spread_root) / 2.0, 0.5, (1.0 + spread_root) / 2.0, 1.0]
    table = [[0.0] * 5 for blank in range(5)]
    for column in range(5):
        coeffs = [1.0]
        divisor = 1.0
        for other_node in range(5):
            if other_node != column:
                product = [0.0] * (len(coeffs) + 1)
                for power, entry in enumerate(coeffs):
                    product[power + 1] += entry
                    product[power] -= node_times[other_node] * entry
                coeffs = product
                divisor *= node_times[column] - node_times[other_node]
        for row_index in range(5):
            upper = node_times[row_index]
            total_sum = 0.0
            for power, entry in enumerate(coeffs):
                total_sum += entry / (power + 1) * upper ** (power + 1)
            table[row_index][column] = total_sum / divisor
    return (np.array(node_times), np.array(table))


def rates(below, here, above, feed, drain):
    rows, lanes = here[0].shape

    def lap(i):
        w = here[i]
        around = (pltpu.roll(w, 1, 0) + pltpu.roll(w, rows - 1, 0)) + (
            pltpu.roll(w, 1, 1) + pltpu.roll(w, lanes - 1, 1)
        )
        return around + (below[i] + above[i]) - 6.0 * w

    s, c = here
    reacting = s * c * c
    grow_sub = substrate_spread * lap(0) - reacting + feed * (1.0 - s)
    grow_cat = catalyst_spread * lap(1) + reacting - drain * c
    return grow_sub, grow_cat


def kernel(
    slabs, blocks, weights,
    guess, feed_in, kill_in,
    end_out, last_out, rate_out,
    u, last, feed, drain, fbuf,
    load_sem, fixed_sem, tm_send, tm_recv, halo_send, halo_recv, cast_send, cast_recv,
):
    layers = guess.shape[2]
    rows = guess.shape[3]
    tm = lax.axis_index("tm")
    sp = lax.axis_index("space")
    left = lax.rem(sp + blocks - 1, blocks)
    right = lax.rem(sp + 1, blocks)
    top = slabs // 2 - 1
    a = tm // 2
    b = tm % 2
    source = tm == slabs - 1
    not_source = tm < slabs - 1
    primary = 1 - b

    def layer_of(c):
        half = c // 2
        odd = c % 2
        return half + odd * (layers - 1 - 2 * half)

    loads = [
        pltpu.make_async_copy(guess, u.at[0, :, :, pl.ds(1, layers)], load_sem.at[0]),
        pltpu.make_async_copy(feed_in, feed, load_sem.at[1]),
        pltpu.make_async_copy(kill_in, drain, load_sem.at[2]),
    ]
    for load in loads:
        load.start()

    def fixed(k):
        return pltpu.make_async_copy(guess.at[0], u.at[k, 0, :, pl.ds(1, layers)], fixed_sem.at[k - 1])

    @pl.when(tm == 0)
    def _():
        for k in range(1, SWEEPS + 1):
            fixed(k).start()

    barrier = pltpu.get_barrier_semaphore()
    for hop in (1, 2, slabs - 2, slabs - 1):
        pl.semaphore_signal(barrier, inc=1, device_id={"tm": lax.rem(tm + hop, slabs)}, device_id_type=MESH)
    for side in (left, right):
        pl.semaphore_signal(barrier, inc=1, device_id={"space": side}, device_id_type=MESH)
    pl.semaphore_wait(barrier, 6)

    def stream(k, c, src):
        return pltpu.make_async_remote_copy(
            src_ref=src,
            dst_ref=u.at[k + 1, 0, :, 1 + layer_of(c)],
            send_sem=tm_send.at[k, c],
            recv_sem=tm_recv.at[k, c],
            device_id={"tm": lax.rem(tm + 1, slabs)},
            device_id_type=MESH,
        )

    def halo(k, side, src):
        return pltpu.make_async_remote_copy(
            src_ref=src,
            dst_ref=u.at[k, :, :, (1 - side) * (layers + 1)],
            send_sem=halo_send.at[k, side],
            recv_sem=halo_recv.at[k, side],
            device_id={"space": left + side * (right - left)},
            device_id_type=MESH,
        )

    def own_edge(k, side):
        return u.at[k, :, :, 1 + side * (layers - 1)]

    halo(0, 0, guess.at[:, :, 0]).start()
    halo(0, 1, guess.at[:, :, layers - 1]).start()

    @pl.when(not_source)
    def _():
        @pl.loop(0, layers)
        def _(c):
            stream(0, c, guess.at[4, :, layer_of(c)]).start()

    for load in loads:
        load.wait()
    drain[...] = drain[...] + feed[...]

    @pl.when(tm == 0)
    def _():
        for k in range(1, SWEEPS + 1):
            fixed(k).wait()

    def arrive(k, c):
        @pl.when(c == 0)
        def _():
            halo(k, 1, own_edge(k, 1)).wait_recv()

        @pl.when(c == 1)
        def _():
            halo(k, 0, own_edge(k, 0)).wait_recv()

    def begin(k, c):
        @pl.when(tm > 0)
        def _():
            stream(k, c, u.at[k, 4, :, 1 + layer_of(c)]).wait_recv()

    def all_rates(k, i):
        f, d = feed[i], drain[i]
        for j in range(5):
            below, here, above = ((u[k, j, 0, i + n], u[k, j, 1, i + n]) for n in range(3))
            fbuf[j, 0], fbuf[j, 1] = rates(below, here, above, f, d)

    def step(k, i, nodes):
        @pl.loop(0, rows // 8)
        def _(r):
            at = pl.ds(pl.multiple_of(r * 8, 8), 8)
            for s in range(2):
                start = u[k + 1, 0, s, 1 + i, at]
                grown = [fbuf[j, s, at] for j in range(5)]
                for m in nodes:
                    total = grown[0] * weights[m][0]
                    for j in range(1, 5):
                        total = total + grown[j] * weights[m][j]
                    u[k + 1, m, s, 1 + i, at] = start + total

    @pl.loop(0, SWEEPS - 1)
    def _(k):
        @pl.loop(0, layers)
        def _(c):
            i = layer_of(c)
            arrive(k, c)
            all_rates(k, i)
            begin(k, c)
            step(k, i, (4, 1, 2, 3))

            @pl.when(not_source)
            def _():
                stream(k + 1, c, u.at[k + 1, 4, :, 1 + i]).start()

            @pl.when(c < 2)
            def _():
                halo(k + 1, c, own_edge(k + 1, c)).start()

    def cast(lane, c, species, target):
        at = last.at[species, 1 + layer_of(c)]
        return pltpu.make_async_remote_copy(
            src_ref=at,
            dst_ref=at,
            send_sem=cast_send.at[lane, c],
            recv_sem=cast_recv.at[species, c],
            device_id={"tm": target},
            device_id_type=MESH,
        )

    down_on = a > 0
    cross_on = (a < top) | source
    cross_species = primary + jnp.where(source, 1, 0)
    extra_on = tm == 2 * (top - 1)

    def down(c):
        return cast(0, c, primary, lax.rem(tm + slabs - 2, slabs))

    def cross(c):
        return cast(1, c, cross_species, tm + 1 - 2 * b)

    def extra(c):
        return cast(2, c, 0, lax.rem(tm + 2, slabs))

    def last_halo(side):
        return pltpu.make_async_remote_copy(
            src_ref=last.at[:, 1 + side * (layers - 1)],
            dst_ref=last.at[:, (1 - side) * (layers + 1)],
            send_sem=halo_send.at[SWEEPS, side],
            recv_sem=halo_recv.at[SWEEPS, side],
            device_id={"space": left + side * (right - left)},
            device_id_type=MESH,
        )

    @pl.loop(0, layers + LAG)
    def _(c):
        @pl.when(c < layers)
        def _():
            i = layer_of(c)
            arrive(SWEEPS - 1, c)
            all_rates(SWEEPS - 1, i)
            begin(SWEEPS - 1, c)
            step(SWEEPS - 1, i, (4,))
            end_out[:, i] = u[SWEEPS, 4, :, 1 + i]

            @pl.when(source)
            def _():
                last[:, 1 + i] = u[SWEEPS, 4, :, 1 + i]

            @pl.when(not_source)
            def _():
                cast(0, c, primary, tm).wait_recv()

            @pl.when(down_on)
            def _():
                down(c).start()

            @pl.when(cross_on)
            def _():
                cross(c).start()

        @pl.when((c >= LAG) & extra_on)
        def _():
            late = c - LAG
            cast(0, late, 1 - primary, tm).wait_recv()
            extra(late).start()

    def rest(first, stop):
        @pl.when(not_source & (tm != 2 * (top - 1)))
        def _():
            @pl.loop(first, stop)
            def _(c):
                cast(0, c, 1 - primary, tm).wait_recv()

    rest(0, 2)
    last_halo(0).start()
    last_halo(1).start()
    rest(2, layers)
    last_halo(0).wait_recv()
    last_halo(1).wait_recv()

    @pl.loop(0, layers)
    def _(i):
        below, here, above = ((last[0, i + n], last[1, i + n]) for n in range(3))
        grow = rates(below, here, above, feed[i], drain[i])
        for s in range(2):
            last_out[s, i] = here[s]
            rate_out[s, i] = slab_time * grow[s]

    for k in range(SWEEPS):
        for side in range(2):
            halo(k, side, own_edge(k, side)).wait_send()
    last_halo(0).wait_send()
    last_halo(1).wait_send()

    @pl.loop(0, layers)
    def _(c):
        @pl.when(not_source)
        def _():
            for k in range(SWEEPS):
                stream(k, c, u.at[k, 4, :, 1 + layer_of(c)]).wait_send()

        @pl.when(down_on)
        def _():
            down(c).wait_send()

        @pl.when(cross_on)
        def _():
            cross(c).wait_send()

        @pl.when(extra_on)
        def _():
            extra(c).wait_send()


def shards(slabs, blocks, guess, feed_rate, kill_rate):
    node_times, table = lobatto_table()
    weights = [[float(np.float32(slab_time * w)) for w in row] for row in table]
    _, nodes, species, layers, rows, lanes = guess.shape
    pair = jax.ShapeDtypeStruct((species, layers, rows, lanes), jnp.float32)
    dma = pltpu.SemaphoreType.DMA
    end, last, rate = pl.pallas_call(
        functools.partial(kernel, slabs, blocks, weights),
        out_shape=(pair, pair, pair),
        in_specs=[pl.BlockSpec(memory_space=pltpu.HBM)] * 3,
        out_specs=(pl.BlockSpec(memory_space=pltpu.VMEM),) * 3,
        scratch_shapes=[
            pltpu.VMEM((SWEEPS + 1, nodes, species, layers + 2, rows, lanes), jnp.float32),
            pltpu.VMEM((species, layers + 2, rows, lanes), jnp.float32),
            pltpu.VMEM((layers, rows, lanes), jnp.float32),
            pltpu.VMEM((layers, rows, lanes), jnp.float32),
            pltpu.VMEM((nodes, species, rows, lanes), jnp.float32),
            dma((3,)),
            dma((SWEEPS,)),
            dma((SWEEPS, layers)),
            dma((SWEEPS, layers)),
            dma((SWEEPS + 1, 2)),
            dma((SWEEPS + 1, 2)),
            dma((3, layers)),
            dma((2, layers)),
        ],
        compiler_params=pltpu.CompilerParams(
            collective_id=0, has_side_effects=True, vmem_limit_bytes=40 * 1024 * 1024
        ),
    )(guess[0], feed_rate, kill_rate)
    offsets = jnp.asarray(node_times, jnp.float32).reshape((-1, 1, 1, 1, 1))
    next_one = last[None] + offsets * rate[None]
    return (end[None], next_one[None])


def solution(mesh):
    placed = (
        P("tm", None, None, "space", None, None),
        P("space", None, None),
        P("space", None, None),
    )
    return jax.shard_map(
        functools.partial(shards, mesh.shape["tm"], mesh.shape["space"]),
        mesh=mesh,
        in_specs=placed,
        out_specs=(P("tm", None, "space", None, None), P("tm", None, None, "space", None, None)),
        check_vma=False,
    )
```
